32 devices in a mesh: member: 2 (over core), dp: 16 (over z, y, x).
Axes of the slice: x: 2, y: 2, z: 4, core: 2. Of those that a mesh axis runs over, the one named last changes fastest.
Arguments:
- features: float32 [4, 256, 16, 256], P('member', 'dp'), may hold values from -6 to 6
- actions: int32 [4, 256, 16], P('member', 'dp'), may hold values from 0 to 127
- advantages: float32 [4, 256, 16], P('member', 'dp'), may hold values from -6 to 6
- h_start: float32 [4, 256, 256], P('member', 'dp'), may hold values from -0.9 to 0.9
- c_start: float32 [4, 256, 256], P('member', 'dp'), may hold values from -4 to 4
- w_lstm: float32 [4, 512, 1024], P('member'), may hold values from -0.25 to 0.25
- b_lstm: float32 [4, 1024], P('member'), may hold values from -3 to 3
- w_head: float32 [4, 256, 128], P('member'), may hold values from -1.875 to 1.875
- head_bias: float32 [4, 128], P('member'), may hold values from -3 to 330
- m_lstm: float32 [4, 512, 1024], P('member', 'dp'), may hold values from -0.06 to 0.06
- m_bias: float32 [4, 1024], P('member', 'dp'), may hold values from -0.06 to 0.06
- m_head: float32 [4, 256, 128], P('member', 'dp'), may hold values from -0.06 to 0.06
- m_head_bias: float32 [4, 128], P('member', 'dp'), may hold values from -0.06 to 0.06
- v_lstm: float32 [4, 512, 1024], P('member', 'dp'), may hold values from 1e-05 to 0.001
- v_bias: float32 [4, 1024], P('member', 'dp'), may hold values from 1e-05 to 0.001
- v_head: float32 [4, 256, 128], P('member', 'dp'), may hold values from 1e-05 to 0.001
- v_head_bias: float32 [4, 128], P('member', 'dp'), may hold values from 1e-05 to 0.001
- winners: int32 [4], replicated, may hold values from 0 to 3
- exploit_flags: int32 [4], replicated, may hold values 0 or 1
Outputs:
- new_w_lstm: float32 [4, 512, 1024], P('member')
- new_b_lstm: float32 [4, 1024], P('member')
- new_w_head: float32 [4, 256, 128], P('member')
- new_head_bias: float32 [4, 128], P('member')
- new_m_lstm: float32 [4, 512, 1024], P('member', 'dp')
- new_m_bias: float32 [4, 1024], P('member', 'dp')
- new_m_head: float32 [4, 256, 128], P('member', 'dp')
- new_m_head_bias: float32 [4, 128], P('member', 'dp')
- new_v_lstm: float32 [4, 512, 1024], P('member', 'dp')
- new_v_bias: float32 [4, 1024], P('member', 'dp')
- new_v_head: float32 [4, 256, 128], P('member', 'dp')
- new_v_head_bias: float32 [4, 128], P('member', 'dp')
The draws below stay inside these ranges and needn't reach their ends.
All inputs are finite; a program needn't handle non-finite values.
Results may differ from the reference program's by a relative error of at most 0.0003.
Values sent between devices are 32-bit elements; how exact they have to be, the bound alone decides.
No kernel may reach another device: no remote copies, remote signals or barrier semaphores. Data moves between devices by JAX's collectives and lax.ppermute only.
A program may use at most 64 MiB of HBM per device.

```python
import math
import jax
import jax.numpy as jnp
from jax import lax

IN = 256
H = 256
ACT = 128
B_DEV = 16
TSTEPS = 16
AGENTS = 4
SEQS = 256


def draw_head_bias(key, part):
    k_base = jax.random.fold_in(key, 0)
    return jnp.clip(jax.random.normal(k_base, (AGENTS, ACT), jnp.float32), -3.0, 3.0)


def place_ends(values, own_key, smallest, high):
    dims = values.shape
    place = [jax.random.randint(jax.random.fold_in(own_key, axis), (), 0, dims[axis]) for axis in range(len(dims))]
    values = values.at[tuple(place)].set(smallest)
    longest = dims.index(max(dims))
    place[longest] = (place[longest] + 1) % dims[longest]
    return values.at[tuple(place)].set(high)


def block_levels(rng, shape, pieces, least, largest):
    def one(position, parts):
        draws = jax.random.uniform(jax.random.fold_in(jax.random.fold_in(rng, 6), position), (parts,), jnp.float32, least / len(pieces), largest / len(pieces))
        return jnp.repeat(jnp.exp(draws), shape[position] // parts).reshape((-1,) + (1,) * (len(shape) - position - 1))

    loudness = one(*pieces[0])
    for cut in pieces[1:]:
        loudness = loudness * one(*cut)
    return loudness


def noise(rng, dims, scale, reach, pieces=(), kind=jnp.bfloat16):
    factor_of = block_levels(rng, dims, pieces, -0.22, 0.18) if pieces else 1.0
    values = jax.random.normal(rng, dims, jnp.float32) * scale * factor_of
    return jnp.minimum(jnp.maximum(values, -reach), reach).astype(kind)


def setup_inputs(seed: int = 0) -> dict:
    seeds = jax.random.split(jax.random.key(seed), 20)
    return {
        "features": noise(seeds[0], (AGENTS, SEQS, TSTEPS, IN), 1.0, 6.0, ((0, 2), (1, 16)), jnp.float32),
        "actions": place_ends(jax.random.randint(seeds[1], (AGENTS, SEQS, TSTEPS), 0, ACT), jax.random.fold_in(seeds[1], 1), 0, ACT - 1).astype(jnp.int32),
        "advantages": noise(seeds[2], (AGENTS, SEQS, TSTEPS), 1.0, 6.0, ((0, 2), (1, 16)), jnp.float32),
        "h_start": jnp.clip(jax.random.uniform(seeds[3], (AGENTS, SEQS, H), jnp.float32, -0.9, 0.9) * block_levels(seeds[3], (AGENTS, SEQS, H), ((0, 2), (1, 16)), -0.4, 0.0), -0.9, 0.9),
        "c_start": noise(seeds[4], (AGENTS, SEQS, H), 1.0, 4.0, ((0, 2), (1, 16)), jnp.float32),
        "w_lstm": noise(seeds[5], (AGENTS, IN + H, 4 * H), (IN + H) ** -0.5, 0.25, ((0, 2),), jnp.float32),
        "b_lstm": noise(seeds[6], (AGENTS, 4 * H), 0.5, 3.0, ((0, 2),), jnp.float32),
        "w_head": noise(seeds[7], (AGENTS, H, ACT), (6.0 * H ** -0.5), 1.875, ((0, 2),), jnp.float32),
        "head_bias": draw_head_bias(jax.random.fold_in(seeds[19], 71), 0),
        "m_lstm": noise(seeds[9], (AGENTS, IN + H, 4 * H), 0.01, 0.06, ((0, 2), (1, 16)), jnp.float32),
        "m_bias": noise(seeds[10], (AGENTS, 4 * H), 0.01, 0.06, ((0, 2), (1, 16)), jnp.float32),
        "m_head": noise(seeds[11], (AGENTS, H, ACT), 0.01, 0.06, ((0, 2), (1, 16)), jnp.float32),
        "m_head_bias": noise(seeds[12], (AGENTS, ACT), 0.01, 0.06, ((0, 2), (1, 16)), jnp.float32),
        "v_lstm": jnp.clip(jnp.exp(math.log(0.001) - 4.6051703 * jax.random.uniform(seeds[13], (AGENTS, IN + H, 4 * H), jnp.float32) ** block_levels(seeds[13], (AGENTS, IN + H, 4 * H), ((0, 2), (1, 16)), -0.2, 0.2)), 9.999999747378752e-06, 0.001),
        "v_bias": jnp.clip(jnp.exp(math.log(0.001) - 4.6051703 * jax.random.uniform(seeds[14], (AGENTS, 4 * H), jnp.float32) ** block_levels(seeds[14], (AGENTS, 4 * H), ((0, 2), (1, 16)), -0.2, 0.2)), 9.999999747378752e-06, 0.001),
        "v_head": jnp.clip(jnp.exp(math.log(0.001) - 4.6051703 * jax.random.uniform(seeds[15], (AGENTS, H, ACT), jnp.float32) ** block_levels(seeds[15], (AGENTS, H, ACT), ((0, 2), (1, 16)), -0.2, 0.2)), 9.999999747378752e-06, 0.001),
        "v_head_bias": jnp.clip(jnp.exp(math.log(0.001) - 4.6051703 * jax.random.uniform(seeds[16], (AGENTS, ACT), jnp.float32) ** block_levels(seeds[16], (AGENTS, ACT), ((0, 2), (1, 16)), -0.2, 0.2)), 9.999999747378752e-06, 0.001),
        "winners": place_ends(jax.random.randint(seeds[17], (AGENTS,), 0, AGENTS), jax.random.fold_in(seeds[17], 1), 0, AGENTS - 1).astype(jnp.int32),
        "exploit_flags": place_ends((jax.random.randint(seeds[18], (AGENTS,), 0, 2) < 1).astype(jnp.int32), jax.random.fold_in(seeds[18], 1), 0, 1),
    }


def agent_loss(w_lstm, b_lstm, w_head, head_bias, features, actions, advantages, h_start, c_start):
    hidden = w_head.shape[0]

    def advance(carry, inputs):
        h_state, c_state = carry
        frame, acted, weight = inputs
        joined = jnp.concatenate([frame, h_state], axis=1)
        gates = jnp.dot(joined, w_lstm, precision=lax.Precision.HIGHEST) + b_lstm
        in_gate = jax.nn.sigmoid(gates[:, 0:hidden])
        forget = jax.nn.sigmoid(gates[:, hidden:2 * hidden])
        cell_in = jnp.tanh(gates[:, 2 * hidden:3 * hidden])
        out_gate = jax.nn.sigmoid(gates[:, 3 * hidden:])
        c_state = forget * c_state + in_gate * cell_in
        h_state = out_gate * jnp.tanh(c_state)
        logits = jnp.dot(h_state, w_head, precision=lax.Precision.HIGHEST) + head_bias
        top = lax.optimization_barrier(jnp.max(logits, axis=1, keepdims=True))
        total = jnp.log(lax.optimization_barrier(jnp.sum(jnp.exp(logits - top), axis=1))) + top[:, 0]
        picked = lax.optimization_barrier(jnp.sum(jnp.where(jnp.arange(logits.shape[1])[None, :] == acted[:, None], logits, 0.0), axis=1))
        return ((h_state, c_state), jnp.sum(weight * (total - picked)))
    frames = jnp.transpose(features, (1, 0, 2))
    acts = jnp.transpose(actions, (1, 0))
    weights = jnp.transpose(advantages, (1, 0))
    carry, terms = lax.scan(advance, (h_start, c_start), (frames, acts, weights))
    return jnp.sum(terms) / (B_DEV * TSTEPS)

def adam_update(param, first, second, grad):
    first = 0.9 * first + 0.1 * grad
    second = 0.999 * second + 0.001 * grad * grad
    param = param - 0.01 * first / (jnp.sqrt(second) + 1e-08)
    return (param, first, second)

def reference(features, actions, advantages, h_start, c_start, w_lstm, b_lstm, w_head, head_bias, m_lstm, m_bias, m_head, m_head_bias, v_lstm, v_bias, v_head, v_head_bias, winners, exploit_flags):
    grad_fn = jax.grad(agent_loss, argnums=(0, 1, 2, 3))
    params = [w_lstm, b_lstm, w_head, head_bias]
    firsts = [m_lstm, m_bias, m_head, m_head_bias]
    seconds = [v_lstm, v_bias, v_head, v_head_bias]
    for step in range(2):

        def one_agent(items):
            return grad_fn(*items)
        grads = lax.map(one_agent, (params[0], params[1], params[2], params[3], features, actions, advantages, h_start, c_start))
        for k in range(4):
            params[k], firsts[k], seconds[k] = adam_update(params[k], firsts[k], seconds[k], grads[k])
    agents = jnp.arange(winners.shape[0], dtype=jnp.int32)
    source = jnp.where(exploit_flags == 1, winners, agents).astype(jnp.int32)
    result = [x[source] for x in params + firsts + seconds]
    return (result[0], result[1], result[2], result[3], result[4], result[5], result[6], result[7], result[8], result[9], result[10], result[11])
```

```python
import functools
import jax
import jax.numpy as jnp
from jax import lax
from jax.experimental import pallas as pl
from jax.experimental.pallas import tpu as pltpu
from jax.sharding import Mesh, PartitionSpec as P

F32 = jnp.float32
BF16 = jnp.bfloat16
LOSS_SCALE = 1.0 / 256.0
QUAD = 4
NN = ((1,), (0,))
NT = ((1,), (1,))
TN = ((0,), (0,))
VMEM_LIMIT = 56 << 20


def split(x):
    hi = x.astype(BF16)
    return hi, (x - hi.astype(F32)).astype(BF16)


def mm(a, b, dims):
    return lax.dot_general(a, b, (dims, ((), ())), preferred_element_type=F32)


def dot3(a, b, dims):
    return mm(a[0], b[0], dims) + (mm(a[1], b[0], dims) + mm(a[0], b[1], dims))


def dot3_few(a, b, dims):
    n = a[0].shape[0]
    r = mm(jnp.concatenate([a[0], a[1]], 0), b[0], dims)
    return r[:n] + (r[n:] + mm(a[0], b[1], dims))


class Sizes:
    def __init__(self, R, rows, wide, hid, act):
        self.R, self.rows, self.wide, self.hid, self.act = R, rows, wide, hid, act
        D = QUAD * R
        self.B = rows // D
        self.half = self.B // 2
        self.W = QUAD * self.half
        self.h = hid // D // 2
        self.CH = self.W + 8
        self.b_each = wide // D
        self.hb_each = act // D
        self.bl = wide // 2


def own_bias(S, r):
    at = lax.broadcasted_iota(jnp.int32, (2, S.bl), 0) * S.bl + lax.broadcasted_iota(jnp.int32, (2, S.bl), 1)
    return ((at // S.b_each) & (S.R - 1)) == r


def own_head_bias(S, r):
    at = lax.broadcasted_iota(jnp.int32, (1, S.act), 1)
    return ((at // S.hb_each) & (S.R - 1)) == r


def grad_kernel(S, T, packed, *refs):
    who, x_ref = refs[0], refs[1]
    n_in = 2 * S.R if packed else 4
    w_in = refs[2 : 2 + n_in]
    keep, send = refs[2 + n_in : 4 + n_in]
    (xs, zx, gi, gf, gg, go, tc, cp, hs, dhh, lgs, dzh, dzl, whi, wlo, ws, whs, bs, hbs) = refs[4 + n_in :]
    c, r = who[0], who[1]
    nb = x_ref.shape[2]
    IN = x_ref.shape[3]
    H = S.hid
    N = QUAD * nb
    rows_all = T * N
    R, B, half, W, h = S.R, S.B, S.half, S.W, S.h

    if packed:
        rel_of = bit_orders(R)
        bias = jnp.zeros((2, S.bl), F32)
        hbias = jnp.zeros((1, S.act), F32)
        for i in range(2 * R):
            mine = i < R
            ref = w_in[i]
            hc = c if mine else 1 - c
            rel = jnp.where(hc == 0, rel_of[0][i % R], rel_of[1][i % R])
            src = r ^ rel
            for z in range(QUAD):
                at = pl.multiple_of((z * R + src) * B + hc * half, half)
                ws[pl.ds(at, half), :] = ref[z * half : (z + 1) * half, :]
                at = pl.multiple_of(((z * R + src) * 2 + hc) * h, h)
                whs[pl.ds(at, h), :] = ref[W : W + h, z * S.act : (z + 1) * S.act]
            bias += jnp.where(hc == 0, ref[W : W + 2, S.bl :], 0.0)
            hbias += jnp.where(hc == 0, ref[W + 2 : W + 3, S.bl : S.bl + S.act], 0.0)
        bs[:, 0 : S.bl] = bias[0:1]
        bs[:, S.bl :] = bias[1:2]
        hbs[...] = hbias
        w_ref, b_ref, wh_ref, hb_ref = ws, bs, whs, hbs
    else:
        w_ref, b_ref, wh_ref, hb_ref = w_in
    hi, lo = split(w_ref[...])
    whi[...] = hi
    wlo[...] = lo

    for z in range(QUAD):
        xs[:, z] = x_ref[z, 0:T]
    xv = split(xs[...].reshape(rows_all, IN))
    zx[...] = dot3(xv, (whi[0:IN], wlo[0:IN]), NN) + b_ref[...]
    h0 = x_ref[:, T].reshape(N, IN)
    c0 = x_ref[:, T + 1].reshape(N, IN)
    aux = x_ref[:, T + 2].reshape(N, IN)

    def forward(t, carry):
        hv, cv = carry
        at = pl.ds(pl.multiple_of(t * N, N), N)
        hs[at, :] = hv
        cp[at, :] = cv
        z = zx[at, :] + dot3_few(split(hv), (whi[IN:], wlo[IN:]), NN)
        i = jax.nn.sigmoid(z[:, 0:H])
        f = jax.nn.sigmoid(z[:, H : 2 * H])
        g = jnp.tanh(z[:, 2 * H : 3 * H])
        o = jax.nn.sigmoid(z[:, 3 * H :])
        cv = f * cv + i * g
        th = jnp.tanh(cv)
        gi[at, :] = i
        gf[at, :] = f
        gg[at, :] = g
        go[at, :] = o
        tc[at, :] = th
        return o * th, cv

    hv, _ = lax.fori_loop(0, T, forward, (h0, c0))
    hs[rows_all : rows_all + N, :] = hv

    hh = split(hs[N : rows_all + N, :])
    whp = split(wh_ref[...])
    lgs[...] = dot3(hh, whp, NN) + hb_ref[...]
    lane = lax.broadcasted_iota(jnp.int32, (N, S.act), 1).astype(F32)
    for t in range(T):
        lg = lgs[t * N : (t + 1) * N, :]
        e = jnp.exp(lg - jnp.max(lg, axis=1, keepdims=True))
        p = e / jnp.sum(e, axis=1, keepdims=True)
        hot = jnp.where(lane == aux[:, T + t : T + t + 1], 1.0, 0.0)
        lgs[t * N : (t + 1) * N, :] = (aux[:, t : t + 1] * LOSS_SCALE) * (p - hot)
    dl = lgs[...]
    d_hb = jnp.sum(dl, axis=0, keepdims=True)
    dls = split(dl)
    d_wh = dot3(hh, dls, TN)
    dhh[...] = dot3(dls, whp, NT)

    def backward(k, carry):
        rec, dc = carry
        t = T - 1 - k
        at = pl.ds(pl.multiple_of(t * N, N), N)
        i, f, g, o, th = gi[at, :], gf[at, :], gg[at, :], go[at, :], tc[at, :]
        dh = dhh[at, :] + rec
        dc = dc + dh * o * (1.0 - th * th)
        dz = jnp.concatenate(
            [
                dc * g * (i * (1.0 - i)),
                dc * cp[at, :] * (f * (1.0 - f)),
                dc * i * (1.0 - g * g),
                dh * th * (o * (1.0 - o)),
            ],
            axis=1,
        )
        zh, zl = split(dz)
        dzh[at, :] = zh
        dzl[at, :] = zl
        zx[at, :] = dz
        return dot3_few((zh, zl), (whi[IN:], wlo[IN:]), NT), dc * f

    zero = jnp.zeros((N, H), F32)
    lax.fori_loop(0, T, backward, (zero, zero))
    d_b = jnp.sum(zx[...], axis=0, keepdims=True)

    first = c == 0
    dz = (dzh[...], dzl[...])
    span = R * B
    for z in range(QUAD):
        lo_row = z * span
        if lo_row < IN:
            left = (xv[0][:, lo_row : lo_row + span], xv[1][:, lo_row : lo_row + span])
        else:
            left = split(hs[0:rows_all, lo_row - IN : lo_row - IN + span])
        dw = dot3(left, dz, TN)
        for rr in range(R):
            a = dw[rr * B : rr * B + half]
            b = dw[rr * B + half : (rr + 1) * B]
            keep[rr, z * half : (z + 1) * half, :] = jnp.where(first, a, b)
            send[rr, z * half : (z + 1) * half, :] = jnp.where(first, b, a)
    d_b2 = jnp.concatenate([d_b[:, 0 : S.bl], d_b[:, S.bl :]], axis=0)
    for rr in range(R):
        for ref in (keep, send):
            ref[rr, W:, :] = jnp.zeros((8, S.wide), F32)
            ref[rr, W : W + 2, S.bl :] = jnp.where(own_bias(S, rr), d_b2, 0.0)
            ref[rr, W + 2 : W + 3, S.bl : S.bl + S.act] = jnp.where(own_head_bias(S, rr), d_hb, 0.0)
        for z in range(QUAD):
            at = (z * R + rr) * 2 * h
            a = d_wh[at : at + h]
            b = d_wh[at + h : at + 2 * h]
            keep[rr, W : W + h, z * S.act : (z + 1) * S.act] = jnp.where(first, a, b)
            send[rr, W : W + h, z * S.act : (z + 1) * S.act] = jnp.where(first, b, a)


def bit_orders(R):
    bits = [1 << s for s in range(R.bit_length() - 1)]
    orders = []
    for order in (bits, bits[::-1]):
        rels = [0]
        for b in order:
            rels += [x ^ b for x in rels]
        orders.append(rels)
    return orders


def grads_call(S, T, packed, who, x, weights):
    nb, IN = x.shape[2], x.shape[3]
    N = QUAD * nb
    rows = T * N
    V = pltpu.VMEM
    chunk = jax.ShapeDtypeStruct((S.R, S.CH, S.wide), F32)
    gate = V((rows, S.hid), F32)
    wide16 = V((rows, S.wide), BF16)
    w16 = V((S.rows, S.wide), BF16)
    n_in = len(weights)
    flops = 2 * rows * S.wide * (S.rows + S.rows + S.hid) * 3
    return pl.pallas_call(
        functools.partial(grad_kernel, S, T, packed),
        out_shape=(chunk, chunk),
        in_specs=[pl.BlockSpec(memory_space=pltpu.SMEM)] + [pl.BlockSpec(memory_space=pltpu.VMEM)] * (1 + n_in),
        out_specs=[pl.BlockSpec(memory_space=pltpu.VMEM)] * 2,
        scratch_shapes=[
            V((T, QUAD, nb, IN), F32),
            V((rows, S.wide), F32),
            gate, gate, gate, gate, gate, gate,
            V((rows + N, S.hid), F32),
            gate,
            V((rows, S.act), F32),
            wide16, wide16, w16, w16,
            V((S.rows, S.wide), F32),
            V((S.hid, S.act), F32),
            V((1, S.wide), F32),
            V((1, S.act), F32),
        ],
        compiler_params=pltpu.CompilerParams(vmem_limit_bytes=VMEM_LIMIT),
        cost_estimate=pl.CostEstimate(flops=flops * 8, transcendentals=rows * S.hid * 5, bytes_accessed=8 << 20),
        name="lstm_grads",
    )(who, x, *weights)


def adam(p, m, v, g):
    m = 0.9 * m + 0.1 * g
    v = 0.999 * v + 0.001 * g * g
    return p - 0.01 * m / (jnp.sqrt(v) + 1e-08), m, v


def total(parts):
    g = parts[0]
    for i in range(1, parts.shape[0]):
        g = g + parts[i]
    return g


def first_adam_kernel(S, who, g_ref, w_ref, b_ref, wh_ref, hb_ref, mv0, mv1, mv2, mv3, p_out, m_out, v_out):
    c, r, q = who[0], who[1], who[2]
    W, half, h, B, R = S.W, S.half, S.h, S.B, S.R
    for ref in (p_out, m_out, v_out):
        ref[W:, :] = jnp.zeros((8, S.wide), F32)
    moments = (mv0, mv1, mv2, mv3)

    def put(at, lanes, new):
        for ref, x in zip((p_out, m_out, v_out), new):
            ref[at, lanes] = x

    every = slice(None)
    mb = jnp.zeros((2, S.bl), F32)
    vb, mhb, vhb = mb, jnp.zeros((1, S.act), F32), jnp.zeros((1, S.act), F32)
    for s in range(QUAD):
        z = (q - s) & (QUAD - 1)
        ref = moments[s]
        at = pl.ds(pl.multiple_of(z * half, half), half)
        g = g_ref[0, at, :]
        for i in range(1, R):
            g = g + g_ref[i, at, :]
        p = w_ref[pl.ds(pl.multiple_of((z * R + r) * B + c * half, half), half), :]
        put(at, every, adam(p, ref[0:half, :], ref[half:B, :], g))
        lanes = pl.ds(pl.multiple_of(z * S.act, S.act), S.act)
        at = slice(W, W + h)
        g = g_ref[0, at, lanes]
        for i in range(1, R):
            g = g + g_ref[i, at, lanes]
        p = wh_ref[pl.ds(pl.multiple_of(((z * R + r) * 2 + c) * h, h), h), :]
        put(at, lanes, adam(p, ref[B : B + h, 0 : S.act], ref[B : B + h, S.act : 2 * S.act], g))
        mb = mb + ref[B : B + 2, S.bl :]
        vb = vb + ref[B + 2 : B + 4, S.bl :]
        mhb = mhb + ref[B + 4 : B + 5, S.bl : S.bl + S.act]
        vhb = vhb + ref[B + 5 : B + 6, S.bl : S.bl + S.act]
    b2 = jnp.concatenate([b_ref[:, 0 : S.bl], b_ref[:, S.bl :]], axis=0)
    p = jnp.where(own_bias(S, r), b2, 0.0)
    put(slice(W, W + 2), slice(S.bl, None), adam(p, mb, vb, total(g_ref[:, W : W + 2, S.bl :])))
    p = jnp.where(own_head_bias(S, r), hb_ref[...], 0.0)
    lanes = slice(S.bl, S.bl + S.act)
    put(slice(W + 2, W + 3), lanes, adam(p, mhb, vhb, total(g_ref[:, W + 2 : W + 3, lanes])))


def second_adam_kernel(S, g_ref, p_ref, m_ref, v_ref, p_out, mv_out):
    W, half, h, B = S.W, S.half, S.h, S.B
    p, m, v = adam(p_ref[...], m_ref[...], v_ref[...], total(g_ref[...]))
    p_out[...] = p
    for z in range(QUAD):
        mv_out[z, 0:half, :] = m[z * half : (z + 1) * half]
        mv_out[z, half:B, :] = v[z * half : (z + 1) * half]
        mv_out[z, B:, :] = jnp.zeros((8, S.wide), F32)
        mv_out[z, B : B + h, 0 : S.act] = m[W : W + h, z * S.act : (z + 1) * S.act]
        mv_out[z, B : B + h, S.act : 2 * S.act] = v[W : W + h, z * S.act : (z + 1) * S.act]
        mv_out[z, B : B + 2, S.bl :] = m[W : W + 2, S.bl :]
        mv_out[z, B + 2 : B + 4, S.bl :] = v[W : W + 2, S.bl :]
        mv_out[z, B + 4 : B + 5, S.bl : S.bl + S.act] = m[W + 2 : W + 3, S.bl : S.bl + S.act]
        mv_out[z, B + 5 : B + 6, S.bl : S.bl + S.act] = v[W + 2 : W + 3, S.bl : S.bl + S.act]


def vmem_call(fn, name, out_shape, smem, *args):
    specs = [pl.BlockSpec(memory_space=pltpu.SMEM)] * smem
    specs += [pl.BlockSpec(memory_space=pltpu.VMEM)] * (len(args) - smem)
    return pl.pallas_call(
        fn,
        out_shape=out_shape,
        in_specs=specs,
        out_specs=jax.tree.map(lambda _: pl.BlockSpec(memory_space=pltpu.VMEM), out_shape),
        compiler_params=pltpu.CompilerParams(vmem_limit_bytes=VMEM_LIMIT),
        name=name,
    )(*args)


def unpack_kernel(S, L, who, *refs):
    c, r = who[0], who[1]
    pieces = refs[: 2 * S.R]
    w_out, b_out, wh_out, hb_out = refs[2 * S.R :]
    R, B, half, W, h = S.R, S.B, S.half, S.W, S.h
    rel_of = bit_orders(R)
    for l in range(L):
        bias = jnp.zeros((2, S.bl), F32)
        hbias = jnp.zeros((1, S.act), F32)
        for i in range(2 * R):
            hc = c if i < R else 1 - c
            src = r ^ jnp.where(c == 0, rel_of[0][i % R], rel_of[1][i % R])
            ref = pieces[i]
            for z in range(QUAD):
                at = pl.multiple_of((z * R + src) * B + hc * half, half)
                w_out[l, pl.ds(at, half), :] = ref[l, z * half : (z + 1) * half, :]
                at = pl.multiple_of(((z * R + src) * 2 + hc) * h, h)
                wh_out[l, pl.ds(at, h), :] = ref[l, W : W + h, z * S.act : (z + 1) * S.act]
            if i < R:
                bias = bias + ref[l, W : W + 2, S.bl :]
                hbias = hbias + ref[l, W + 2 : W + 3, S.bl : S.bl + S.act]
        b_out[l : l + 1, 0 : S.bl] = bias[0:1]
        b_out[l : l + 1, S.bl :] = bias[1:2]
        hb_out[l : l + 1, :] = hbias


def swap_cores(x):
    return lax.ppermute(x, "c", [(0, 1), (1, 0)])


def gather_columns(R, arrays):
    bits = [1 << s for s in range(R.bit_length() - 1)]
    held = [list(arrays)]
    for up, down in zip(bits, bits[::-1]):
        pairs = [(j, j ^ up) for j in range(R)] + [(R + j, R + (j ^ down)) for j in range(R)]
        held += [[lax.ppermute(x, ("c", "r"), pairs) for x in xs] for xs in held]
    return held


def pick(options, index):
    out = options[-1]
    for i in range(len(options) - 2, -1, -1):
        out = jnp.where(index == i, options[i], out)
    return out


def local(K, R, features, actions, advantages, h_start, c_start, w_lstm, b_lstm, w_head, head_bias,
          m_lstm, m_bias, m_head, m_head_bias, v_lstm, v_bias, v_head, v_head_bias, winners, exploit_flags):
    L, n, T, IN = features.shape
    S = Sizes(R, w_lstm.shape[1], w_lstm.shape[2], w_head.shape[1], w_head.shape[2])
    k, c, q, r = (lax.axis_index(a).astype(jnp.int32) for a in "kcqr")
    D = QUAD * R
    d = q * R + r
    who = jnp.stack([c, r, q])

    mine = (q >> 1) == c
    state = (w_lstm, b_lstm.reshape(L, 1, -1), w_head, head_bias.reshape(L, 1, -1))
    ours = [lax.dynamic_index_in_dim(x, q & 1, 0, keepdims=False) for x in state]
    weights = [jnp.where(mine, x, swap_cores(x)) for x in ours]

    aux = jnp.concatenate([advantages, actions.astype(F32)], axis=2)
    aux = jnp.pad(aux, ((0, 0), (0, 0), (0, IN - 2 * T)))
    seq = jnp.concatenate(
        [features.transpose(0, 2, 1, 3), h_start[:, None], c_start[:, None], aux[:, None]], axis=1
    ).reshape(L, T + 3, 2, n // 2, IN)
    here = lax.dynamic_index_in_dim(seq, c, 2, keepdims=False)
    there = swap_cores(lax.dynamic_index_in_dim(seq, 1 - c, 2, keepdims=False))
    x = jnp.concatenate([jnp.where(c == 0, here, there), jnp.where(c == 0, there, here)], axis=0)
    x = lax.all_to_all(x, "q", 0, 0, tiled=True)

    lanes = jnp.arange(S.wide, dtype=jnp.int32)

    def spread(b, each):
        width = b.shape[1] * D
        return jnp.where(lanes[:width] // each == d, jnp.tile(b, (1, D)), 0.0)

    def rest(m, v, mb, vb, mhb, vhb, side):
        heads = jnp.concatenate([lax.dynamic_slice_in_dim(a, side * S.h, S.h, 1) for a in (m, v)], axis=2)
        heads = jnp.pad(heads, ((0, 0), (0, 8 - S.h), (0, S.bl - 2 * S.act)))
        hb = jnp.pad(jnp.stack([spread(mhb, S.hb_each), spread(vhb, S.hb_each)], axis=1), ((0, 0), (0, 2), (0, S.bl - S.act)))
        biases = [spread(a, S.b_each).reshape(L, 2, S.bl) for a in (mb, vb)]
        return jnp.concatenate([heads, jnp.concatenate(biases + [hb], axis=1)], axis=2)

    def moment_block(side):
        rows = [lax.dynamic_slice_in_dim(a, side * S.half, S.half, 1) for a in (m_lstm, v_lstm)]
        extra = rest(m_head, v_head, m_bias, v_bias, m_head_bias, v_head_bias, side)
        return jnp.concatenate(rows + [extra], axis=1)

    here = moment_block(c)
    there = swap_cores(moment_block(1 - c))
    blocks = jnp.concatenate([jnp.where(c == 0, here, there), jnp.where(c == 0, there, here)], axis=0)
    moments = [lax.dynamic_index_in_dim(blocks, q, 0, keepdims=False)]
    for s in range(1, QUAD):
        block = lax.dynamic_index_in_dim(blocks, (q + s) & (QUAD - 1), 0, keepdims=False)
        moments.append(lax.ppermute(block, "q", [(i, (i + s) % QUAD) for i in range(QUAD)]))

    chunk = jax.ShapeDtypeStruct((S.CH, S.wide), F32)

    def reduced(keep, send):
        return lax.all_to_all(keep + swap_cores(send), "r", 0, 0, tiled=True)

    g = reduced(*grads_call(S, T, False, who, x, weights))
    p, m, v = vmem_call(
        functools.partial(first_adam_kernel, S), "first_adam", (chunk, chunk, chunk), 1, who, g, *weights, *moments
    )
    held = [a for [a] in gather_columns(R, [p])]
    held += [swap_cores(a) for a in held]
    g = reduced(*grads_call(S, T, True, who, x, held))
    block = jax.ShapeDtypeStruct((QUAD, S.B + 8, S.wide), F32)
    p, mv = vmem_call(functools.partial(second_adam_kernel, S), "second_adam", (chunk, block), 0, g, p, m, v)

    everyone = jnp.arange(winners.shape[0], dtype=jnp.int32)
    source = jnp.where(exploit_flags == 1, winners, everyone)

    def source_of(side, l):
        a = (2 * k + side) * L + l
        return jnp.sum(jnp.where(everyone == a, source, 0))

    def chosen(by_agent, side):
        return jnp.stack([by_agent(source_of(side, l)) for l in range(L)])

    shifted = [p] + [lax.ppermute(p, "q", [(i, (i + s) % QUAD) for i in range(QUAD)]) for s in range(1, QUAD)]
    if K > 1:
        groups = lax.all_gather(jnp.stack(shifted), "k")

        def weights_of(a):
            return lax.dynamic_index_in_dim(groups.reshape(K * QUAD, S.CH, S.wide), (a >> 2) * QUAD + ((q - a) & 3), 0, keepdims=False)
    else:

        def weights_of(a):
            return pick(shifted, (q - a) & 3)

    here = chosen(weights_of, c)
    there = swap_cores(chosen(weights_of, 1 - c))
    held = gather_columns(R, [here, there])
    pieces = [a for a, _ in held] + [b for _, b in held]

    f = lambda *dims: jax.ShapeDtypeStruct(dims, F32)
    new_w, new_b, new_wh, new_hb = vmem_call(
        functools.partial(unpack_kernel, S, L), "unpack",
        (f(L, S.rows, S.wide), f(L, S.wide), f(L, S.hid, S.act), f(L, S.act)), 1, who, *pieces,
    )

    mv = lax.all_to_all(mv, "q", 0, 0, tiled=True)
    if K > 1:
        mv = lax.all_gather(mv, "k").reshape(K * QUAD, S.B + 8, S.wide)

    def moments_of(a):
        return lax.dynamic_index_in_dim(mv, a, 0, keepdims=False)

    here = chosen(moments_of, c)
    there = swap_cores(chosen(moments_of, 1 - c))
    lo, hi = jnp.where(c == 0, here, there), jnp.where(c == 0, there, here)
    B, half, h = S.B, S.half, S.h
    out = []
    for i in range(2):
        rows = jnp.concatenate([a[:, i * half : (i + 1) * half] for a in (lo, hi)], axis=1)
        bias = lo[:, B + 2 * i : B + 2 * i + 2, S.bl :].reshape(L, S.wide)
        head = jnp.concatenate([a[:, B : B + h, i * S.act : (i + 1) * S.act] for a in (lo, hi)], axis=1)
        hb = lo[:, B + 4 + i, S.bl : S.bl + S.act]
        out += [
            rows,
            lax.dynamic_slice_in_dim(bias, d * S.b_each, S.b_each, 1),
            head,
            lax.dynamic_slice_in_dim(hb, d * S.hb_each, S.hb_each, 1),
        ]
    return (new_w, new_b, new_wh, new_hb, *out)


def solution(mesh):
    M, D = mesh.shape["member"], mesh.shape["dp"]
    K, R = M // 2, D // QUAD
    inner = Mesh(mesh.devices.reshape(K, 2, QUAD, R), ("k", "c", "q", "r"))
    member, dp = ("k", "c"), ("q", "r")
    full = [P(member, None, None), P(member, None), P(member, None, None), P(member, None)]
    rows = [P(member, dp, None), P(member, dp), P(member, dp, None), P(member, dp)]
    seqs = [P(member, dp, None, None)] + [P(member, dp, None)] * 4
    return jax.shard_map(
        functools.partial(local, K, R),
        mesh=inner,
        in_specs=(*seqs, *full, *rows, *rows, P(), P()),
        out_specs=(*full, *rows, *rows),
        check_vma=False,
    )
```

```python
import functools
import jax
import jax.numpy as jnp
import numpy as np
from jax import lax
from jax.experimental import pallas as pl
from jax.experimental.pallas import tpu as pltpu
from jax.sharding import Mesh, PartitionSpec as P

F32 = jnp.float32
BF16 = jnp.bfloat16
LOSS_SCALE = 1.0 / 256.0
QUAD = 4
NN = ((1,), (0,))
NT = ((1,), (1,))
TN = ((0,), (0,))
VMEM_LIMIT = 56 << 20
SMALL = pl.CostEstimate(flops=1, transcendentals=0, bytes_accessed=1)


class Either:
    def __init__(self, flag, a, b):
        self.flag, self.a, self.b = flag, a, b

    def __getitem__(self, at):
        return jnp.where(self.flag, self.a[at], self.b[at])


def split(x):
    hi = x.astype(BF16)
    return hi, (x - hi.astype(F32)).astype(BF16)


def mm(a, b, dims):
    return lax.dot_general(a, b, (dims, ((), ())), preferred_element_type=F32)


def dot3(a, b, dims):
    return mm(a[0], b[0], dims) + (mm(a[1], b[0], dims) + mm(a[0], b[1], dims))


def dot3_few(a, b, dims):
    n = a[0].shape[0]
    r = mm(jnp.concatenate([a[0], a[1]], 0), b[0], dims)
    return r[:n] + (r[n:] + mm(a[0], b[1], dims))


class Sizes:
    def __init__(self, R, rows, wide, hid, act):
        self.R, self.rows, self.wide, self.hid, self.act = R, rows, wide, hid, act
        D = QUAD * R
        self.B = rows // D
        self.half = self.B // 2
        self.W = QUAD * self.half
        self.h = hid // D // 2
        self.CH = self.W + 8
        self.b_each = wide // D
        self.hb_each = act // D
        self.bl = wide // 2


def own_bias(S, r):
    at = lax.broadcasted_iota(jnp.int32, (2, S.bl), 0) * S.bl + lax.broadcasted_iota(jnp.int32, (2, S.bl), 1)
    return ((at // S.b_each) & (S.R - 1)) == r


def own_head_bias(S, r):
    at = lax.broadcasted_iota(jnp.int32, (1, S.act), 1)
    return ((at // S.hb_each) & (S.R - 1)) == r


def grad_kernel(S, T, packed, *refs):
    who, x_refs = refs[0], refs[1 : 1 + QUAD]
    n_in = 2 * S.R if packed else 8
    w_in = refs[1 + QUAD : 1 + QUAD + n_in]
    refs = refs[1 + QUAD + n_in :]
    keep, send = refs[: S.R], refs[S.R : 2 * S.R]
    (xs, zx, gi, gf, gg, go, tc, cp, hs, dhh, lgs, dzh, dzl, whi, wlo, ws, whs, bs, hbs, sem) = refs[-20:]
    c, r = who[0], who[1]
    nb = x_refs[0].shape[1]
    IN = x_refs[0].shape[2]
    H = S.hid
    N = QUAD * nb
    rows_all = T * N
    R, B, half, W, h = S.R, S.B, S.half, S.W, S.h

    if packed:
        rel_of = bit_orders(R)
        bias = jnp.zeros((2, S.bl), F32)
        hbias = jnp.zeros((1, S.act), F32)
        for i in range(2 * R):
            mine = i < R
            ref = w_in[i]
            hc = c if mine else 1 - c
            rel = jnp.where(hc == 0, rel_of[0][i % R], rel_of[1][i % R])
            src = r ^ rel
            for z in range(QUAD):
                at = pl.multiple_of((z * R + src) * B + hc * half, half)
                ws[pl.ds(at, half), :] = ref[z * half : (z + 1) * half, :]
                at = pl.multiple_of(((z * R + src) * 2 + hc) * h, h)
                whs[pl.ds(at, h), :] = ref[W : W + h, z * S.act : (z + 1) * S.act]
            bias += jnp.where(hc == 0, ref[W : W + 2, S.bl :], 0.0)
            hbias += jnp.where(hc == 0, ref[W + 2 : W + 3, S.bl : S.bl + S.act], 0.0)
        bs[:, 0 : S.bl] = bias[0:1]
        bs[:, S.bl :] = bias[1:2]
        hbs[...] = hbias
        w_ref, b_ref, wh_ref, hb_ref = ws, bs, whs, hbs
    else:
        mine, at = (who[2] >> 1) == c, who[2] & 1

        @pl.when(mine)
        def _():
            pltpu.make_async_copy(w_in[0].at[at], ws, sem).start()

        @pl.when(jnp.logical_not(mine))
        def _():
            pltpu.make_async_copy(w_in[4].at[at], ws, sem).start()

        for i, ref in ((1, bs), (2, whs), (3, hbs)):
            ref[...] = jnp.where(mine, w_in[i][at], w_in[4 + i][at])
        w_ref, b_ref, wh_ref, hb_ref = ws, bs, whs, hbs

    for z in range(QUAD):
        xs[:, z] = x_refs[z][0:T]
    xv = split(xs[...].reshape(rows_all, IN))
    if not packed:
        pltpu.make_async_copy(w_in[0].at[0], ws, sem).wait()
    hi, lo = split(w_ref[...])
    whi[...] = hi
    wlo[...] = lo
    if not packed:
        own = refs[2 * S.R]
        for z in range(QUAD):
            own[z * half : (z + 1) * half, :] = w_ref[pl.ds(pl.multiple_of((z * R + r) * B + c * half, half), half), :]
        own[W:, :] = jnp.zeros((8, S.wide), F32)
        for z in range(QUAD):
            at = pl.multiple_of(((z * R + r) * 2 + c) * h, h)
            own[W : W + h, z * S.act : (z + 1) * S.act] = wh_ref[pl.ds(at, h), :]
        b2 = b_ref[...]
        b2 = jnp.concatenate([b2[:, 0 : S.bl], b2[:, S.bl :]], axis=0)
        own[W : W + 2, S.bl :] = jnp.where(own_bias(S, r), b2, 0.0)
        own[W + 2 : W + 3, S.bl : S.bl + S.act] = jnp.where(own_head_bias(S, r), hb_ref[...], 0.0)

    zx[...] = dot3(xv, (whi[0:IN], wlo[0:IN]), NN) + b_ref[...]
    h0, c0, aux = (jnp.concatenate([x[T + i] for x in x_refs], axis=0) for i in range(3))

    def forward(t, carry):
        hv, cv = carry
        at = pl.ds(pl.multiple_of(t * N, N), N)
        hs[at, :] = hv
        cp[at, :] = cv
        z = zx[at, :] + dot3_few(split(hv), (whi[IN:], wlo[IN:]), NN)
        i = jax.nn.sigmoid(z[:, 0:H])
        f = jax.nn.sigmoid(z[:, H : 2 * H])
        g = jnp.tanh(z[:, 2 * H : 3 * H])
        o = jax.nn.sigmoid(z[:, 3 * H :])
        cv = f * cv + i * g
        th = jnp.tanh(cv)
        gi[at, :] = i
        gf[at, :] = f
        gg[at, :] = g
        go[at, :] = o
        tc[at, :] = th
        return o * th, cv

    hv, _ = lax.fori_loop(0, T, forward, (h0, c0))
    hs[rows_all : rows_all + N, :] = hv

    hh = split(hs[N : rows_all + N, :])
    whp = split(wh_ref[...])
    lgs[...] = dot3(hh, whp, NN) + hb_ref[...]
    lane = lax.broadcasted_iota(jnp.int32, (N, S.act), 1).astype(F32)
    for t in range(T):
        lg = lgs[t * N : (t + 1) * N, :]
        e = jnp.exp(lg - jnp.max(lg, axis=1, keepdims=True))
        p = e / jnp.sum(e, axis=1, keepdims=True)
        hot = jnp.where(lane == aux[:, IN // 2 + t : IN // 2 + t + 1], 1.0, 0.0)
        lgs[t * N : (t + 1) * N, :] = (aux[:, t : t + 1] * LOSS_SCALE) * (p - hot)
    dl = lgs[...]
    d_hb = jnp.sum(dl, axis=0, keepdims=True)
    dls = split(dl)
    whs[...] = dot3(hh, dls, TN)
    dhh[...] = dot3(dls, whp, NT)

    def backward(k, carry):
        rec, dc = carry
        t = T - 1 - k
        at = pl.ds(pl.multiple_of(t * N, N), N)
        i, f, g, o, th = gi[at, :], gf[at, :], gg[at, :], go[at, :], tc[at, :]
        dh = dhh[at, :] + rec
        dc = dc + dh * o * (1.0 - th * th)
        dz = jnp.concatenate(
            [
                dc * g * (i * (1.0 - i)),
                dc * cp[at, :] * (f * (1.0 - f)),
                dc * i * (1.0 - g * g),
                dh * th * (o * (1.0 - o)),
            ],
            axis=1,
        )
        zh, zl = split(dz)
        dzh[at, :] = zh
        dzl[at, :] = zl
        zx[at, :] = dz
        return dot3_few((zh, zl), (whi[IN:], wlo[IN:]), NT), dc * f

    zero = jnp.zeros((N, H), F32)
    lax.fori_loop(0, T, backward, (zero, zero))
    d_b = jnp.sum(zx[...], axis=0, keepdims=True)

    dz = (dzh[...], dzl[...])
    span = R * B
    for z in range(QUAD):
        lo_row = z * span
        if lo_row < IN:
            left = (xv[0][:, lo_row : lo_row + span], xv[1][:, lo_row : lo_row + span])
        else:
            left = split(hs[0:rows_all, lo_row - IN : lo_row - IN + span])
        ws[lo_row : lo_row + span, :] = dot3(left, dz, TN)
    d_b2 = jnp.concatenate([d_b[:, 0 : S.bl], d_b[:, S.bl :]], axis=0)
    for rel in range(R):
        column = r ^ rel
        d_b_own = jnp.where(own_bias(S, column), d_b2, 0.0)
        d_hb_own = jnp.where(own_head_bias(S, column), d_hb, 0.0)
        for ref, side in ((keep[rel], c), (send[rel], 1 - c)):
            for z in range(QUAD):
                at = pl.multiple_of((z * R + column) * B + side * half, half)
                ref[z * half : (z + 1) * half, :] = ws[pl.ds(at, half), :]
            ref[W:, :] = jnp.zeros((8, S.wide), F32)
            ref[W : W + 2, S.bl :] = d_b_own
            ref[W + 2 : W + 3, S.bl : S.bl + S.act] = d_hb_own
            for z in range(QUAD):
                at = pl.multiple_of(((z * R + column) * 2 + side) * h, h)
                ref[W : W + h, z * S.act : (z + 1) * S.act] = whs[pl.ds(at, h), :]


def bit_orders(R):
    bits = [1 << s for s in range(R.bit_length() - 1)]
    orders = []
    for order in (bits, bits[::-1]):
        rels = [0]
        for b in order:
            rels += [x ^ b for x in rels]
        orders.append(rels)
    return orders


def grads_call(S, T, packed, who, x, weights):
    nb, IN = x[0].shape[1], x[0].shape[2]
    N = QUAD * nb
    rows = T * N
    V = pltpu.VMEM
    chunk = jax.ShapeDtypeStruct((S.CH, S.wide), F32)
    gate = V((rows, S.hid), F32)
    wide16 = V((rows, S.wide), BF16)
    w16 = V((S.rows, S.wide), BF16)
    n_in, n_out = len(weights), 2 * S.R + (0 if packed else 1)
    flops = 2 * rows * S.wide * (S.rows + S.rows + S.hid) * 3
    return pl.pallas_call(
        functools.partial(grad_kernel, S, T, packed),
        out_shape=[chunk] * n_out,
        in_specs=[pl.BlockSpec(memory_space=pltpu.SMEM)]
        + [pl.BlockSpec(memory_space=pltpu.VMEM)] * QUAD
        + [pl.BlockSpec(memory_space=pl.ANY if not packed and i % 4 == 0 else pltpu.VMEM) for i in range(n_in)],
        out_specs=[pl.BlockSpec(memory_space=pltpu.VMEM)] * n_out,
        scratch_shapes=[
            V((T, QUAD, nb, IN), F32),
            V((rows, S.wide), F32),
            gate, gate, gate, gate, gate, gate,
            V((rows + N, S.hid), F32),
            gate,
            V((rows, S.act), F32),
            wide16, wide16, w16, w16,
            V((S.rows, S.wide), F32),
            V((S.hid, S.act), F32),
            V((1, S.wide), F32),
            V((1, S.act), F32),
            pltpu.SemaphoreType.DMA,
        ],
        compiler_params=pltpu.CompilerParams(vmem_limit_bytes=VMEM_LIMIT),
        cost_estimate=pl.CostEstimate(flops=flops * 8, transcendentals=rows * S.hid * 5, bytes_accessed=8 << 20),
        name="lstm_grads",
    )(who, *x, *weights)


def adam(p, m, v, g):
    m = 0.9 * m + 0.1 * g
    v = 0.999 * v + 0.001 * g * g
    return p - 0.01 * m / (jnp.sqrt(v) + 1e-08), m, v


def total(parts):
    g = parts[0][...]
    for part in parts[1:]:
        g = g + part[...]
    return g


def put_gradient_blocks(S, q, g, outs):
    W, half, h = S.W, S.half, S.h
    for s, out in enumerate(outs):
        z = (q + s) & (QUAD - 1)
        out[0:half, :] = g[pl.ds(pl.multiple_of(z * half, half), half), :]
        out[half:, :] = g[W:, :]
        out[half : half + h, 0 : S.act] = g[W : W + h, pl.ds(pl.multiple_of(z * S.act, S.act), S.act)]


def first_adam_kernel(S, who, *refs):
    g_refs, p_ref, moments = refs[: S.R + 1], refs[S.R + 1], refs[S.R + 2 : S.R + 2 + QUAD]
    p_out, m_out, v_out = refs[S.R + 2 + QUAD : S.R + 5 + QUAD]
    g_outs, g_ref = refs[S.R + 5 + QUAD : -1], refs[-1]
    q = who[2]
    W, half, h, B = S.W, S.half, S.h, S.B
    g = total(g_refs)
    g_ref[...] = g
    put_gradient_blocks(S, q, g_ref, g_outs)
    mb = jnp.zeros((2, S.bl), F32)
    vb, mhb, vhb = mb, jnp.zeros((1, S.act), F32), jnp.zeros((1, S.act), F32)
    m_out[W:, :] = jnp.zeros((8, S.wide), F32)
    v_out[W:, :] = jnp.zeros((8, S.wide), F32)
    for s in range(QUAD):
        z = (q - s) & (QUAD - 1)
        ref = moments[s]
        at = pl.ds(pl.multiple_of(z * half, half), half)
        m_out[at, :] = ref[0:half, :]
        v_out[at, :] = ref[half:B, :]
        lanes = pl.ds(pl.multiple_of(z * S.act, S.act), S.act)
        m_out[W : W + h, lanes] = ref[B : B + h, 0 : S.act]
        v_out[W : W + h, lanes] = ref[B : B + h, S.act : 2 * S.act]
        mb = mb + ref[B : B + 2, S.bl :]
        vb = vb + ref[B + 2 : B + 4, S.bl :]
        mhb = mhb + ref[B + 4 : B + 5, S.bl : S.bl + S.act]
        vhb = vhb + ref[B + 5 : B + 6, S.bl : S.bl + S.act]
    m_out[W : W + 2, S.bl :] = mb
    v_out[W : W + 2, S.bl :] = vb
    m_out[W + 2 : W + 3, S.bl : S.bl + S.act] = mhb
    v_out[W + 2 : W + 3, S.bl : S.bl + S.act] = vhb
    p_out[...], m_out[...], v_out[...] = adam(p_ref[...], m_out[...], v_out[...], g)


def second_adam_kernel(S, who, *refs):
    g_refs, (p_ref, m_ref, v_ref, p_out), g_outs, g_ref = refs[: S.R + 1], refs[S.R + 1 : S.R + 5], refs[S.R + 5 : -1], refs[-1]
    g = total(g_refs)
    g_ref[...] = g
    p_out[...] = adam(p_ref[...], m_ref[...], v_ref[...], g)[0]
    put_gradient_blocks(S, who[2], g_ref, g_outs)


def moments_kernel(S, who, here, there, *refs):
    first, second, out = refs[:QUAD], refs[QUAD : 2 * QUAD], refs[2 * QUAD]
    c, q = who[0], who[2]
    half, h, B = S.half, S.h, S.B
    for s in range(QUAD):
        j = (q - s) & (QUAD - 1)
        blocks = Either((j >> 1) == c, here, there)

        def put(m_at, m_lanes, v_at, v_lanes, g_at, g_lanes):
            m, v = blocks[j & 1, m_at, m_lanes], blocks[j & 1, v_at, v_lanes]
            for ref in (first[s], second[s]):
                _, m, v = adam(0.0, m, v, ref[g_at, g_lanes])
            out[j, m_at, m_lanes] = m
            out[j, v_at, v_lanes] = v

        out[j, B:, :] = jnp.zeros((8, S.wide), F32)
        every, tail, one = slice(None), slice(S.bl, None), slice(S.bl, S.bl + S.act)
        put(slice(0, half), every, slice(half, B), every, slice(0, half), every)
        put(slice(B, B + h), slice(0, S.act), slice(B, B + h), slice(S.act, 2 * S.act), slice(half, half + h), slice(0, S.act))
        put(slice(B, B + 2), tail, slice(B + 2, B + 4), tail, slice(half, half + 2), tail)
        put(slice(B + 4, B + 5), one, slice(B + 5, B + 6), one, slice(half + 2, half + 3), one)


def spread(x, width, d):
    each = x.shape[1]
    lane = lax.broadcasted_iota(jnp.int32, (x.shape[0], width), 1) - d * each
    out = jnp.zeros((x.shape[0], width), F32)
    for i in range(each):
        out = jnp.where(lane == i, x[:, i : i + 1], out)
    return out


def pack_moments_kernel(S, who, m, v, mh, vh, mb, vb, mhb, vhb, here, there):
    c, d = who[0], who[2] * S.R + who[1]
    L, B, half, h = m.shape[0], S.B, S.half, S.h
    biases = [spread(x[...], S.wide, d) for x in (mb, vb)]
    head_biases = [spread(x[...], S.act, d) for x in (mhb, vhb)]
    for l in range(L):
        for ref, side in ((here, c), (there, 1 - c)):
            at = pl.ds(pl.multiple_of(side * half, half), half)
            ref[l, 0:half, :] = m[l, at, :]
            ref[l, half:B, :] = v[l, at, :]
            ref[l, B:, :] = jnp.zeros((8, S.wide), F32)
            at = pl.ds(pl.multiple_of(side * h, h), h)
            ref[l, B : B + h, 0 : S.act] = mh[l, at, :]
            ref[l, B : B + h, S.act : 2 * S.act] = vh[l, at, :]
            for i in range(2):
                ref[l, B + 2 * i : B + 2 * i + 1, S.bl :] = biases[i][l : l + 1, 0 : S.bl]
                ref[l, B + 2 * i + 1 : B + 2 * i + 2, S.bl :] = biases[i][l : l + 1, S.bl :]
                ref[l, B + 4 + i : B + 5 + i, S.bl : S.bl + S.act] = head_biases[i][l : l + 1]


def route_kernel(who, here, there, *outs):
    c, q = who[0], who[2]
    for s, out in enumerate(outs):
        j = (q + s) & (QUAD - 1)
        out[...] = Either((j >> 1) == c, here, there)[j & 1]


def choose_kernel(slots, n, L, who, *refs):
    pieces, out, sem = refs[: slots * n], refs[slots * n], refs[slots * n + 1]
    for i in range(n):
        for l in range(L):
            for j in range(slots):

                @pl.when(who[3 + L + l] == j)
                def _():
                    pltpu.make_async_copy(pieces[j * n + i], out.at[i, l], sem.at[i, l]).start()

    for i in range(n):
        for l in range(L):
            pltpu.make_async_copy(pieces[i], out.at[i, l], sem.at[i, l]).wait()


def pack_kernel(T, who, x_ref, h_ref, c_ref, adv_ref, act_ref, here, there):
    L, _, _, IN = x_ref.shape
    nb = here.shape[2]
    for l in range(L):
        for ref, side in ((here, who[0]), (there, 1 - who[0])):
            at = pl.ds(pl.multiple_of(side * nb, nb), nb)
            for t in range(T):
                ref[l, t] = x_ref[l, at, t, :]
            ref[l, T] = h_ref[l, at, :]
            ref[l, T + 1] = c_ref[l, at, :]
            ref[l, T + 2] = jnp.zeros((nb, IN), F32)
            ref[l, T + 2, :, 0:T] = adv_ref[l, at, :]
            ref[l, T + 2, :, IN // 2 : IN // 2 + T] = act_ref[l, at, :].astype(F32)


def vmem_call(fn, name, out_shape, smem, *args, scratch=(), cost=SMALL, space=pltpu.VMEM, out_specs=None):
    specs = [pl.BlockSpec(memory_space=pltpu.SMEM)] * smem
    specs += [pl.BlockSpec(memory_space=space)] * (len(args) - smem)
    return pl.pallas_call(
        fn,
        out_shape=out_shape,
        in_specs=specs,
        out_specs=out_specs or jax.tree.map(lambda _: pl.BlockSpec(memory_space=space), out_shape),
        scratch_shapes=scratch,
        cost_estimate=cost,
        compiler_params=pltpu.CompilerParams(vmem_limit_bytes=VMEM_LIMIT),
        name=name,
    )(*args)


def unpack_kernel(S, L, groups, slots, who, *refs):
    R, B, half, W, h = S.R, S.B, S.half, S.W, S.h
    own, other = refs[: slots * R], refs[slots * R : slots * R + len(groups)]
    w_out, b_out, wh_out, hb_out, rest, sem, rest_sem = refs[slots * R + len(groups) :]
    c, r = who[0], who[1]
    rel_of = bit_orders(R)

    def source(i, hc):
        return r ^ jnp.where(hc == 0, rel_of[0][i], rel_of[1][i])

    def copies(piece, l, i, o):
        hc = c if o == 0 else 1 - c
        src = source(i, hc)
        for z in range(QUAD):
            at = pl.multiple_of((z * R + src) * B + hc * half, half)
            yield pltpu.make_async_copy(piece.at[pl.ds(z * half, half)], w_out.at[l, pl.ds(at, half)], sem.at[l, i, o, z])
        yield pltpu.make_async_copy(piece.at[pl.ds(W, 8)], rest.at[l, i, o], rest_sem.at[l, i, o])

    cases = []
    for g, columns in enumerate(groups):
        for at, i in enumerate(columns):
            for l in range(L):
                cases.append((other[g].at[at, l], l, i, 1))
    for l in range(L):
        for i in range(R):
            for j in range(slots):

                @pl.when(who[3 + l] == j)
                def _():
                    for copy in copies(own[j * R + i], l, i, 0):
                        copy.start()

    for case in cases:
        for copy in copies(*case):
            copy.start()
    waits = [list(copies(*case)) for case in cases]
    waits += [list(copies(own[i], l, i, 0)) for l in range(L) for i in range(R)]
    for group in waits:
        group[-1].wait()
    for l in range(L):
        bias = jnp.zeros((2, S.bl), F32)
        hbias = jnp.zeros((1, S.act), F32)
        for i in range(R):
            for o in range(2):
                hc = c if o == 0 else 1 - c
                src = source(i, hc)
                for z in range(QUAD):
                    at = pl.multiple_of(((z * R + src) * 2 + hc) * h, h)
                    wh_out[l, pl.ds(at, h), :] = rest[l, i, o, 0:h, z * S.act : (z + 1) * S.act]
            bias = bias + rest[l, i, 0, 0:2, S.bl :]
            hbias = hbias + rest[l, i, 0, 2:3, S.bl : S.bl + S.act]
        b_out[l : l + 1, 0 : S.bl] = bias[0:1]
        b_out[l : l + 1, S.bl :] = bias[1:2]
        hb_out[l : l + 1, :] = hbias
    for group in waits:
        for copy in group[:-1]:
            copy.wait()


def swap_cores(x):
    return lax.ppermute(x, "c", [(0, 1), (1, 0)])


def next_column(R, x, bits, i):
    up, down = bits[i], bits[-1 - i]
    return lax.ppermute(x, ("c", "r"), [(j, j ^ up) for j in range(R)] + [(R + j, R + (j ^ down)) for j in range(R)])


def gather_columns(R, x):
    bits = [1 << i for i in range(R.bit_length() - 1)]
    held = [x]
    for i in range(len(bits)):
        held += [next_column(R, y, bits, i) for y in held]
    return held


def along(x, pairs):
    return lax.ppermute(x, "q", pairs)


OUTER = [(0, 1), (1, 0), (2, 3), (3, 2)]
INNER = [(1, 2), (2, 1)]
OUTWARD = [(1, 0), (2, 3)]


def send_blocks(blocks):
    return blocks[:1] + [
        lax.ppermute(blocks[s], "q", [(i, (i + s) % QUAD) for i in range(QUAD)]) for s in range(1, QUAD)
    ]


def pick(options, index):
    out = options[-1]
    for i in range(len(options) - 2, -1, -1):
        out = jnp.where(index == i, options[i], out)
    return out


def local(K, R, features, actions, advantages, h_start, c_start, w_lstm, b_lstm, w_head, head_bias,
          m_lstm, m_bias, m_head, m_head_bias, v_lstm, v_bias, v_head, v_head_bias, winners, exploit_flags):
    L, n, T, IN = features.shape
    S = Sizes(R, w_lstm.shape[1], w_lstm.shape[2], w_head.shape[1], w_head.shape[2])
    k, c, q, r = (lax.axis_index(a).astype(jnp.int32) for a in "kcqr")
    D = QUAD * R
    bits = [1 << i for i in range(R.bit_length() - 1)]

    who = jnp.stack([c, r, q])

    part = jax.ShapeDtypeStruct((L, T + 3, n // 2, IN), F32)
    here, there = vmem_call(
        functools.partial(pack_kernel, T), "pack", (part, part), 1, who, features, h_start, c_start, advantages, actions
    )
    there = swap_cores(there)
    there, w_lstm = lax.optimization_barrier((there, w_lstm))
    weights = [w_lstm, b_lstm.reshape(L, 1, -1), w_head, head_bias.reshape(L, 1, -1)]
    weights += [swap_cores(w) for w in weights]
    message = jax.ShapeDtypeStruct(part.shape[1:], F32)
    outgoing = vmem_call(route_kernel, "route", [message] * QUAD, 1, who, here, there)
    x = send_blocks(list(outgoing))
    *weights, m_lstm, v_lstm, winners = lax.optimization_barrier((*weights, m_lstm, v_lstm, winners))

    slot_of = np.array([[0, 1, 2, 3], [1, 0, 2, 3], [3, 2, 0, 1], [3, 2, 1, 0]], np.int32)
    everyone = jnp.arange(winners.shape[0], dtype=jnp.int32)
    agents = 2 * k * L + np.tile(np.arange(L), 2) + L * jnp.where(np.arange(2 * L) < L, c, 1 - c)
    source = jnp.where(exploit_flags == 1, winners, everyone)
    source = jnp.sum(jnp.where(everyone[None] == agents[:, None], source[None], 0), axis=1)
    slot = jnp.sum(jnp.where(jnp.arange(QUAD)[:, None] == q, slot_of, 0), axis=0)
    slot = jnp.sum(jnp.where((source[:, None] & (QUAD - 1)) == np.arange(QUAD), slot[None], 0), axis=1)
    places = slot if K == 1 else jnp.arange(2 * L, dtype=jnp.int32)
    whose = jnp.concatenate([who, places.astype(jnp.int32), source.astype(jnp.int32)])

    part = jax.ShapeDtypeStruct((L, S.B + 8, S.wide), F32)
    m_here, m_there = vmem_call(
        functools.partial(pack_moments_kernel, S), "pack_moments", (part, part), 1,
        who, m_lstm, v_lstm, m_head, v_head, m_bias, v_bias, m_head_bias, v_head_bias,
    )

    m_there = swap_cores(m_there)
    message = jax.ShapeDtypeStruct(part.shape[1:], F32)
    outgoing = vmem_call(route_kernel, "route_moments", [message] * QUAD, 1, who, m_here, m_there)
    *both, whose = lax.optimization_barrier((*x, *weights, *outgoing, whose))
    x, weights, outgoing = both[:QUAD], both[QUAD:-QUAD], both[-QUAD:]

    chunk = jax.ShapeDtypeStruct((S.CH, S.wide), F32)
    block = [jax.ShapeDtypeStruct((S.half + 8, S.wide), F32)] * QUAD

    def reduced(keep, send, later):
        parts = {}
        for rel in range(R - 1, 0, -1):
            other = swap_cores(send[rel])
            if rel == R - 1:
                other, *later = lax.optimization_barrier((other, *later))
            parts[rel] = lax.ppermute(keep[rel] + other, "r", [(j, j ^ rel) for j in range(R)])
        return [keep[0], swap_cores(send[0])] + [parts[rel] for rel in range(1, R)], send_blocks(later)

    *g, p = grads_call(S, T, False, who, x, weights)
    g, moments = reduced(g[:R], g[R:], outgoing)
    p, m, v, *g = vmem_call(
        functools.partial(first_adam_kernel, S), "first_adam", [chunk] * 3 + block, 1,
        who, *g, p, *moments, scratch=[pltpu.VMEM((S.CH, S.wide), F32)],
    )
    held = gather_columns(R, p)
    held += [swap_cores(a) for a in held]
    g_out = g
    g = grads_call(S, T, True, who, x, held)
    g, g_first = reduced(g[:R], g[R:], g_out)
    p, *g_out = vmem_call(functools.partial(second_adam_kernel, S), "second_adam", [chunk] + block, 1, who, *g, p, m, v,
                           scratch=[pltpu.VMEM((S.CH, S.wide), F32)])

    outer, inner = [p], [p]
    steps = [
        lambda: [along(p, OUTER), along(p, INNER)],
        lambda: [along(inner[1], OUTWARD), along(outer[1], INNER)],
        lambda: [along(inner[2], OUTWARD)],
    ]
    middle = (q == 1) | (q == 2)
    arrivals = [
        lambda: p,
        lambda: outer[1],
        lambda: jnp.where(middle, inner[1], outer[2]),
        lambda: jnp.where(middle, inner[2], outer[3]),
    ]

    own = []
    starts = [QUAD - 1] * QUAD if K > 1 else list(range(QUAD))
    for t in range(starts[-1] + len(bits)):
        if K == 1 and t < QUAD:
            own.append([arrivals[t]()])
        if K > 1 and t == QUAD - 1:
            groups = lax.all_gather(jnp.stack([f() for f in arrivals]), "k").reshape(K * QUAD, S.CH, S.wide)
            for i in range(2 * L):
                at = (source[i] // QUAD) * QUAD + slot[i]
                own.append([lax.dynamic_index_in_dim(groups, at, 0, keepdims=False)])
        moved = steps[t]() if t < QUAD - 1 else []
        n_steps = len(moved)
        for j, held in enumerate(own):
            if 0 <= t - starts[j] < len(bits):
                moved += [next_column(R, x, bits, t - starts[j]) for x in held]
        if t == QUAD - 2:
            g_second = send_blocks(g_out)
            moved += g_second
        if t == QUAD - 1:
            mv = vmem_call(
                functools.partial(moments_kernel, S), "moments", jax.ShapeDtypeStruct((QUAD, S.B + 8, S.wide), F32), 1,
                who, m_here, m_there, *g_first, *g_second,
            )
            if K > 1:
                mv = lax.all_gather(mv, "k").reshape(K * QUAD, S.B + 8, S.wide)
            chosen = [
                jnp.stack([lax.dynamic_index_in_dim(mv, source[side * L + l].astype(jnp.uint32), 0, keepdims=False) for l in range(L)])
                for side in range(2)
            ]
            moved += chosen
        before = [x for held in own for x in held]
        if t < starts[-1] + len(bits) - 1:
            moved = list(lax.optimization_barrier((*moved, *before, *g_out)))
            before = moved[len(moved) - len(before) - QUAD : len(moved) - QUAD]
            g_out = moved[len(moved) - QUAD :]
        for j, held in enumerate(own):
            own[j] = [before.pop(0) for _ in held]
        for path, _ in zip((outer, inner), range(n_steps)):
            path.append(moved.pop(0))
        for j, held in enumerate(own):
            if 0 <= t - starts[j] < len(bits):
                held += [moved.pop(0) for _ in list(held)]
        if t == QUAD - 2:
            g_second = [moved.pop(0) for _ in range(QUAD)]
        if t == QUAD - 1:
            chosen = [moved.pop(0) for _ in range(2)]
            mv_there = swap_cores(chosen[1])

    f = lambda *dims: jax.ShapeDtypeStruct(dims, F32)
    columns = [list(range(R // 2)), list(range(R // 2, R))]
    vm = pl.BlockSpec(memory_space=pltpu.VMEM)
    other = []
    for group in columns:
        pieces = [held[i] for held in own for i in group]
        out = vmem_call(
            functools.partial(choose_kernel, len(own), len(group), L), "choose", f(len(group), L, S.CH, S.wide), 1,
            whose, *pieces, space=pl.ANY, out_specs=vm, scratch=[pltpu.SemaphoreType.DMA((len(group), L))],
        )
        other.append(swap_cores(out))
    new_w, new_b, new_wh, new_hb = vmem_call(
        functools.partial(unpack_kernel, S, L, columns, len(own)), "unpack",
        (f(L, S.rows, S.wide), f(L, S.wide), f(L, S.hid, S.act), f(L, S.act)), 1,
        whose, *[a for held in own for a in held], *other, space=pl.ANY,
        out_specs=(vm, vm, vm, vm),
        scratch=[pltpu.VMEM((L, R, 2, 8, S.wide), F32), pltpu.SemaphoreType.DMA((L, R, 2, QUAD)),
                 pltpu.SemaphoreType.DMA((L, R, 2))],
    )

    here, there = chosen[0], mv_there
    lo, hi = jnp.where(c == 0, here, there), jnp.where(c == 0, there, here)
    B, half, h = S.B, S.half, S.h
    d = (q * R + r).astype(jnp.uint32)
    out = []
    for i in range(2):
        rows = jnp.concatenate([a[:, i * half : (i + 1) * half] for a in (lo, hi)], axis=1)
        bias = lo[:, B + 2 * i : B + 2 * i + 2, S.bl :].reshape(L, S.wide)
        head = jnp.concatenate([a[:, B : B + h, i * S.act : (i + 1) * S.act] for a in (lo, hi)], axis=1)
        hb = lo[:, B + 4 + i, S.bl : S.bl + S.act]
        out += [
            rows,
            lax.dynamic_slice_in_dim(bias, d * S.b_each, S.b_each, 1),
            head,
            lax.dynamic_slice_in_dim(hb, d * S.hb_each, S.hb_each, 1),
        ]
    return (new_w, new_b, new_wh, new_hb, *out)


def solution(mesh):
    M, D = mesh.shape["member"], mesh.shape["dp"]
    K, R = M // 2, D // QUAD
    inner = Mesh(mesh.devices.reshape(K, 2, QUAD, R), ("k", "c", "q", "r"))
    member, dp = ("k", "c"), ("q", "r")
    full = [P(member, None, None), P(member, None), P(member, None, None), P(member, None)]
    rows = [P(member, dp, None), P(member, dp), P(member, dp, None), P(member, dp)]
    seqs = [P(member, dp, None, None)] + [P(member, dp, None)] * 4
    return jax.shard_map(
        functools.partial(local, K, R),
        mesh=inner,
        in_specs=(*seqs, *full, *rows, *rows, P(), P()),
        out_specs=(*full, *rows, *rows),
        check_vma=False,
    )
```
